32 devices in a mesh: gx: 2 (over y), gy: 4 (over x, core), gz: 4 (over z).
Axes of the slice: x: 2, y: 2, z: 4, core: 2. Of those that a mesh axis runs over, the one named last changes fastest.
Arguments:
- snapshots: bfloat16 [16, 64, 64, 256], P('gx', 'gy', 'gz'), may hold values from -1500 to 1500
- sketch: float32 [256, 256], replicated, may hold values from -0.5 to 1.5
- velocity: float32 [3, 16, 64, 64], P(None, 'gx', 'gy', 'gz'), may hold values from -4 to 4
- viscosity: float32 [16, 64, 64], P('gx', 'gy', 'gz'), may hold values from 0.2 to 2
Outputs:
- applied_modes: bfloat16 [16, 64, 64, 256], P('gx', 'gy', 'gz')
- reduced: float32 [256, 256], replicated
The draws below stay inside these ranges and needn't reach their ends.
All inputs are finite; a program needn't handle non-finite values.
Results may differ from the reference program's by a relative error of at most 0.0015.
The reference program's roundings to bfloat16 on the way (of `sketched`) count: a program that leaves them out, or rounds other values in their place, can miss the bound.
Values may be sent and summed in bfloat16 or wider, within the bound.
No kernel may reach another device: no remote copies, remote signals or barrier semaphores. Data moves between devices by JAX's collectives and lax.ppermute only.
A program may use at most 64 MiB of HBM per device.

```python
import math
import jax
import jax.numpy as jnp
from jax import lax

R = 256
CX = 8
CY = 16
CZ = 16
NX = 16
NY = 64
NZ = 64


heavy_factor = 6.0


def heavy_region():
    in_x = (jnp.arange(NX) < CX).reshape(NX, 1, 1, 1)
    in_y = (jnp.arange(NY) < CY).reshape(1, NY, 1, 1)
    in_z = (jnp.arange(NZ) < 2 * CZ).reshape(1, 1, NZ, 1)
    inside = jnp.logical_and(jnp.logical_and(in_x, in_y), in_z)
    return jnp.where(inside, heavy_factor, 1.0).astype(jnp.float32)


def draw_snapshots(key, part):
    keys = jax.random.split(key, 1)
    position = (jnp.arange(NX, dtype=jnp.float32) / max(NX - 1, 1)).reshape(NX, 1, 1, 1)
    base_values = jnp.clip(jax.random.normal(keys[0], (NX, NY, NZ, R), jnp.float32), -6.0, 6.0)
    ramp = jnp.exp(0.5 * math.log(3.0) * position)
    values = base_values * ramp
    values = values * heavy_region()
    return values.astype(jnp.bfloat16)


def draw_sketch(key, part):
    spread = jnp.clip(jax.random.normal(key, (R, R), jnp.float32), -6.0, 6.0)
    return jnp.eye(R, dtype=jnp.float32) + 0.5 / math.sqrt(R) * spread


def block_levels(key, extent, shards, least, top_value):
    level, own = 1.0, jax.random.fold_in(key, 6)
    for dim, blocks in shards:
        heights = jnp.exp(jax.random.uniform(jax.random.fold_in(own, dim), (blocks,), jnp.float32, least / len(shards), top_value / len(shards)))
        level = level * jnp.repeat(heights, extent[dim] // blocks).reshape([-1 if axis == dim else 1 for axis in range(len(extent))])
    return level


def scatter_about(rng, shape, scale, most, cuts=(), held_as=jnp.bfloat16):
    array = scale * jax.random.normal(rng, shape, jnp.float32)
    if cuts:
        array = array * block_levels(rng, shape, cuts, -0.22, 0.18)
    return jnp.clip(array, -most, most).astype(held_as)


def setup_inputs(seed: int = 0) -> dict:
    splits = jax.random.split(jax.random.key(seed), 5)
    snapshots = draw_snapshots(jax.random.fold_in(splits[4], 71), 0)
    sketch = draw_sketch(jax.random.fold_in(splits[4], 71), 0)
    velocity = scatter_about(splits[2], (3, NX, NY, NZ), 1.0, 4.0, ((1, 2), (2, 4), (3, 4)), jnp.float32)
    viscosity = jnp.clip(jnp.exp(math.log(2.0) - 2.3025851 * jax.random.uniform(splits[3], (NX, NY, NZ), jnp.float32) ** block_levels(splits[3], (NX, NY, NZ), ((0, 2), (1, 4), (2, 4)), -0.2, 0.2)), 0.2, 2.0)
    return dict(snapshots=snapshots, sketch=sketch, velocity=velocity, viscosity=viscosity)


def plane_operator(before_plane, middle, after_plane, velocity_plane, viscous_plane):
    padded = jnp.pad(middle, ((1, 1), (1, 1), (0, 0)))
    north_side = padded[2:, 1:-1]
    south_side = padded[:-2, 1:-1]
    upper_side = padded[1:-1, 2:]
    lower_side = padded[1:-1, :-2]
    neighbours = after_plane + before_plane + north_side + south_side + upper_side + lower_side
    viscous_term = viscous_plane[..., None] * (6.0 * middle - neighbours)
    flow_term = velocity_plane[0][..., None] * (after_plane - before_plane)
    flow_term = flow_term + velocity_plane[1][..., None] * (north_side - south_side)
    flow_term = flow_term + velocity_plane[2][..., None] * (upper_side - lower_side)
    return viscous_term + 0.5 * flow_term

def reference(snapshots, sketch, velocity, viscosity):
    highest = lax.Precision.HIGHEST

    def project_plane(plane_in):
        flat_rows = plane_in.reshape(-1, R).astype(jnp.float32)
        return jnp.dot(flat_rows, sketch, precision=highest).astype(jnp.bfloat16).reshape(NY, NZ, R)
    sketched = lax.map(project_plane, snapshots)

    def gram_step(running, plane_in):
        flat_rows = plane_in.reshape(-1, R)
        return (running + jnp.dot(flat_rows.T.astype(jnp.float32), flat_rows.astype(jnp.float32), preferred_element_type=jnp.float32), None)
    gram_matrix, unused = lax.scan(gram_step, jnp.zeros((R, R), jnp.float32), sketched)
    total_cells = NX * NY * NZ
    gram_matrix = gram_matrix / total_cells
    lower_factor = jnp.linalg.cholesky(gram_matrix)
    inverse = jax.scipy.linalg.solve_triangular(lower_factor, jnp.eye(R, dtype=jnp.float32), lower=True)

    def image_step(running, plane_index):
        middle = lax.dynamic_index_in_dim(sketched, plane_index, 0, keepdims=False).astype(jnp.float32)
        earlier = lax.dynamic_index_in_dim(sketched, jnp.maximum(plane_index - 1, 0).astype(jnp.int32), 0, keepdims=False).astype(jnp.float32)
        later = lax.dynamic_index_in_dim(sketched, jnp.minimum(plane_index + 1, NX - 1).astype(jnp.int32), 0, keepdims=False).astype(jnp.float32)
        earlier = jnp.where(plane_index > 0, earlier, jnp.zeros_like(earlier))
        later = jnp.where(plane_index < NX - 1, later, jnp.zeros_like(later))
        velocity_plane = lax.dynamic_index_in_dim(velocity, plane_index, 1, keepdims=False)
        viscous_plane = lax.dynamic_index_in_dim(viscosity, plane_index, 0, keepdims=False)
        applied = plane_operator(earlier, middle, later, velocity_plane, viscous_plane).reshape(-1, R)
        running = running + jnp.dot(middle.reshape(-1, R).T, applied, precision=highest)
        plane_out = jnp.dot(applied, inverse.T, precision=highest).astype(jnp.bfloat16).reshape(NY, NZ, R)
        return (running, plane_out)
    image_gram, applied_modes = lax.scan(image_step, jnp.zeros((R, R), jnp.float32), jnp.arange(NX, dtype=jnp.int32))
    image_gram = image_gram / total_cells
    reduced = jnp.dot(jnp.dot(inverse, image_gram, precision=highest), inverse.T, precision=highest)
    return (applied_modes, reduced)
```

```python
import functools

import jax
import jax.numpy as jnp
from jax import lax
from jax.experimental import pallas as pl
from jax.experimental.pallas import tpu as pltpu
from jax.sharding import PartitionSpec as P

f32 = jnp.float32
bf16 = jnp.bfloat16
VMEM = pl.BlockSpec(memory_space=pltpu.VMEM)


def split3(x):
    high = x.astype(bf16)
    left = x - high.astype(f32)
    middle = left.astype(bf16)
    low = (left - middle.astype(f32)).astype(bf16)
    return high, middle, low


def dot_f32(a, b, dim_a, dim_b):
    ah, am, al = split3(a)
    bh, bm, bl = split3(b)
    left = jnp.concatenate([ah, ah, am, am, ah, al], axis=dim_a)
    right = jnp.concatenate([bh, bm, bh, bm, bl, bh], axis=dim_b)
    return lax.dot_general(
        left, right, (((dim_a,), (dim_b,)), ((), ())), preferred_element_type=f32
    )


def sketch_kernel(scale, snap_ref, sketch_ref, out_ref, gram_ref, parts_ref):
    columns = sketch_ref.shape[0]
    half = columns // 2
    step = pl.program_id(0)

    @pl.when(step == 0)
    def _():
        for i, part in enumerate(split3(sketch_ref[...])):
            parts_ref[i * columns : (i + 1) * columns, :] = part
        gram_ref[...] = jnp.zeros_like(gram_ref)

    rows = snap_ref[...]
    made = jnp.dot(
        jnp.concatenate([rows, rows, rows], axis=1), parts_ref[...], preferred_element_type=f32
    ).astype(bf16)
    out_ref[...] = made
    gram = lax.dot_general(made, made, (((0,), (0,)), ((), ())), preferred_element_type=f32) * scale
    gram_ref[:half, :] += gram[:half, :half]
    gram_ref[half : 2 * half, :] += gram[:half, half:]
    gram_ref[2 * half :, :] += gram[half:, half:]


def sketch_call(rows, sketch, scale):
    count, columns = rows.shape
    steps = 4
    block = count // steps
    half = columns // 2
    return pl.pallas_call(
        functools.partial(sketch_kernel, scale),
        grid=(steps,),
        in_specs=[
            pl.BlockSpec((block, columns), lambda i: (i, 0)),
            pl.BlockSpec((columns, columns), lambda i: (0, 0)),
        ],
        out_specs=[
            pl.BlockSpec((block, columns), lambda i: (i, 0)),
            pl.BlockSpec((3 * half, half), lambda i: (0, 0)),
        ],
        out_shape=[
            jax.ShapeDtypeStruct((count, columns), bf16),
            jax.ShapeDtypeStruct((3 * half, half), f32),
        ],
        scratch_shapes=[pltpu.VMEM((3 * columns, columns), bf16)],
        name="sketch",
    )(rows, sketch)


def operator_kernel(
    scale, s_ref, xm_ref, xp_ref, ym_ref, yp_ref, zm_ref, zp_ref, coef_ref, image_ref, gram_ref
):
    cells_x, cells_y, cells_z, columns = s_ref.shape
    total = jnp.zeros(gram_ref.shape, f32)
    for x in range(cells_x):
        plane = s_ref[x]
        before = (s_ref[x - 1] if x > 0 else xm_ref[0]).astype(f32)
        after = (s_ref[x + 1] if x < cells_x - 1 else xp_ref[0]).astype(f32)
        middle = plane.astype(f32)
        south = jnp.concatenate([ym_ref[x].astype(f32), middle[:-1]], axis=0)
        north = jnp.concatenate([middle[1:], yp_ref[x].astype(f32)], axis=0)
        lower = jnp.concatenate([zm_ref[x].astype(f32), middle[:, :-1]], axis=1)
        upper = jnp.concatenate([middle[:, 1:], zp_ref[x].astype(f32)], axis=1)
        around = (after + before) + (north + south) + (upper + lower)

        def spread(k):
            return jnp.stack([coef_ref[k, x, :, y : y + 1] for y in range(cells_y)], axis=0)

        image = spread(3) * (6.0 * middle - around)
        image = image + spread(0) * (after - before)
        image = image + spread(1) * (north - south)
        image = image + spread(2) * (upper - lower)
        image_ref[x] = image
        flat = image.reshape(-1, columns)
        base = plane.reshape(-1, columns)
        total = total + lax.dot_general(
            jnp.concatenate([base, base, base], axis=0),
            jnp.concatenate(split3(flat), axis=0),
            (((0,), (0,)), ((), ())),
            preferred_element_type=f32,
        )
    gram_ref[...] = total * scale


def operator_call(sketched, halos, coefs, scale):
    columns = sketched.shape[-1]
    return pl.pallas_call(
        functools.partial(operator_kernel, scale),
        in_specs=[VMEM] * 8,
        out_specs=[VMEM] * 2,
        out_shape=[
            jax.ShapeDtypeStruct(sketched.shape, f32),
            jax.ShapeDtypeStruct((columns, columns), f32),
        ],
        name="operator",
    )(sketched, *halos, coefs)


def factor_kernel(nb, g_ref, o_ref, m_ref):
    n = o_ref.shape[0]
    half = n // 2
    m_ref[:half, :half] = g_ref[:half, :]
    m_ref[half:, :half] = jnp.zeros((half, half), f32)
    m_ref[:half, half:] = g_ref[half : 2 * half, :]
    m_ref[half:, half:] = g_ref[2 * half :, :]
    lane = lax.broadcasted_iota(jnp.int32, (nb, n), 1)
    lane_b = lax.broadcasted_iota(jnp.int32, (nb, nb), 1)
    row_b = lax.broadcasted_iota(jnp.int32, (nb, nb), 0)
    rowi = lax.broadcasted_iota(jnp.int32, (nb, 1), 0)
    for r0 in range(0, n, nb):
        end = r0 + nb
        block = m_ref[r0:end, r0:end]
        pivots = jnp.zeros((nb, 1), f32)
        for j in range(nb):
            col = block[:, j : j + 1]
            row = block[j : j + 1, :]
            r = 1.0 / col[j : j + 1, :]
            pivots = jnp.where(rowi == j, r, pivots)
            if j < nb - 1:
                factors = jnp.where(rowi > j, col * r, 0.0)
                block = jnp.where((lane_b == j) & (row_b > j), -factors, block - factors * row)
        unit = jnp.where(lane_b < row_b, block, jnp.where(lane_b == row_b, 1.0, 0.0))
        panel = dot_f32(unit, m_ref[r0:end, :], 1, 0)
        pieces = [unit]
        if r0:
            pieces = [jnp.zeros((nb, r0), f32)] + pieces
        if end < n:
            pieces = pieces + [jnp.zeros((nb, n - end), f32)]
        inside = (lane >= r0) & (lane < end)
        rows = jnp.where(inside, jnp.concatenate(pieces, axis=1), panel)
        o_ref[r0:end, :] = jnp.where(lane < end, rows * jnp.sqrt(pivots), 0.0)
        if end < n:
            factors = (panel * pivots)[:, end:]
            lane_r = lax.broadcasted_iota(jnp.int32, (n - end, n), 1)
            old = jnp.where((lane_r >= r0) & (lane_r < end), 0.0, m_ref[end:, :])
            m_ref[end:, :] = old - dot_f32(factors, rows, 0, 0)


def factor_call(packed):
    n = packed.shape[1] * 2
    return pl.pallas_call(
        functools.partial(factor_kernel, 64),
        in_specs=[VMEM],
        out_specs=VMEM,
        out_shape=jax.ShapeDtypeStruct((n, n), f32),
        scratch_shapes=[pltpu.VMEM((n, n), f32)],
        name="factor",
    )(packed)


def apply_kernel(image_ref, inverse_ref, out_ref):
    out_ref[...] = dot_f32(image_ref[...], inverse_ref[...], 1, 1).astype(bf16)


def apply_call(image, inverse):
    count, columns = image.shape
    steps = 8
    block = count // steps
    return pl.pallas_call(
        apply_kernel,
        grid=(steps,),
        in_specs=[
            pl.BlockSpec((block, columns), lambda i: (i, 0)),
            pl.BlockSpec((columns, columns), lambda i: (0, 0)),
        ],
        out_specs=pl.BlockSpec((block, columns), lambda i: (i, 0)),
        out_shape=jax.ShapeDtypeStruct((count, columns), bf16),
        name="apply",
    )(image, inverse)


def reduce_kernel(inverse_ref, gram_ref, out_ref):
    inverse = inverse_ref[...]
    out_ref[...] = dot_f32(dot_f32(inverse, gram_ref[...], 1, 0), inverse, 1, 1)


def reduce_call(inverse, gram):
    return pl.pallas_call(
        reduce_kernel,
        in_specs=[VMEM] * 2,
        out_specs=VMEM,
        out_shape=jax.ShapeDtypeStruct(gram.shape, f32),
        name="reduced",
    )(inverse, gram)


def swap(value, axes, mask):
    count = lax.axis_size(axes)
    return lax.ppermute(value, axes, [(i, i ^ mask) for i in range(count)])


def all_sum(value):
    plane = ("gx", "gy")
    count = lax.axis_size(plane)
    depth = lax.axis_size("gz")
    half = value.shape[0] // 2
    if count & (count - 1) or depth & (depth - 1) or count < 2 or half % 8:
        return lax.psum(value, ("gx", "gy", "gz"))
    low = lax.axis_index(plane) & 1
    sent = lax.dynamic_slice_in_dim(value, (1 - low) * half, half, 0)
    part = lax.dynamic_slice_in_dim(value, low * half, half, 0) + swap(sent, plane, 1)
    mask = 2
    while mask < count:
        part = part + swap(part, plane, mask)
        mask *= 2
    mask = 1
    while mask < depth:
        part = part + swap(part, "gz", mask)
        mask *= 2
    other = swap(part, plane, 1)
    return jnp.where(
        low == 0, jnp.concatenate([part, other], axis=0), jnp.concatenate([other, part], axis=0)
    )


def halo_pair(cells, axis, dim):
    count = lax.axis_size(axis)
    head = lax.slice_in_dim(cells, 0, 1, axis=dim)
    tail = lax.slice_in_dim(cells, cells.shape[dim] - 1, cells.shape[dim], axis=dim)
    if count == 1:
        return jnp.zeros_like(head), jnp.zeros_like(head)
    even = lax.axis_index(axis) % 2 == 0
    pairs = []
    for i in range(0, count - 1, 2):
        pairs += [(i, i + 1), (i + 1, i)]
    first = lax.ppermute(jnp.where(even, tail, head), axis, pairs)
    pairs = []
    for i in range(1, count - 1, 2):
        pairs += [(i, i + 1), (i + 1, i)]
    second = jnp.zeros_like(first)
    if pairs:
        second = lax.ppermute(jnp.where(even, head, tail), axis, pairs)
    return jnp.where(even, second, first), jnp.where(even, first, second)


def per_device(snapshots, sketch, velocity, viscosity):
    columns = sketch.shape[0]
    shape = snapshots.shape
    ncells = shape[0] * shape[1] * shape[2]
    for axis in ("gx", "gy", "gz"):
        ncells *= lax.axis_size(axis)
    scale = 1.0 / ncells
    sketched, packed = sketch_call(snapshots.reshape(-1, columns), sketch, scale)
    sketched = sketched.reshape(shape)
    inverse = factor_call(all_sum(packed))
    halos = []
    for axis, dim in (("gx", 0), ("gy", 1), ("gz", 2)):
        halos += halo_pair(sketched, axis, dim)
    coefs = jnp.concatenate([0.5 * velocity, viscosity[None]], axis=0).transpose(0, 1, 3, 2)
    image, image_gram = operator_call(sketched, halos, coefs, scale)
    image_gram = all_sum(image_gram)
    applied = apply_call(image.reshape(-1, columns), inverse)
    reduced = reduce_call(inverse, image_gram)
    return applied.reshape(shape), reduced


def solution(mesh):
    in_specs = (P("gx", "gy", "gz", None), P(), P(None, "gx", "gy", "gz"), P("gx", "gy", "gz"))
    out_specs = (P("gx", "gy", "gz", None), P())
    return jax.shard_map(
        per_device, mesh=mesh, in_specs=in_specs, out_specs=out_specs, check_vma=False
    )
```

```python
import functools

import jax
import jax.numpy as jnp
from jax import lax
from jax.experimental import pallas as pl
from jax.experimental.pallas import tpu as pltpu
from jax.sharding import PartitionSpec as P

f32 = jnp.float32
bf16 = jnp.bfloat16
VMEM = pl.BlockSpec(memory_space=pltpu.VMEM)
SMEM = pl.BlockSpec(memory_space=pltpu.SMEM)
HBM = pl.BlockSpec(memory_space=pltpu.HBM)
PARAMS = pltpu.CompilerParams(vmem_limit_bytes=16 << 20)
TILE = 8
PANEL = 64


def split2(x):
    high = x.astype(bf16)
    return high, (x - high.astype(f32)).astype(bf16)


def split3(x):
    high = x.astype(bf16)
    return (high, *split2(x - high.astype(f32)))


def matmul(a, b, dim_a, dim_b):
    return lax.dot_general(a, b, (((dim_a,), (dim_b,)), ((), ())), preferred_element_type=f32)


def dot_f32(a, b, dim_a, dim_b):
    ah, am, al = split3(a)
    bh, bm, bl = split3(b)
    left = jnp.concatenate([ah, ah, am, am, ah, al], axis=dim_a)
    right = jnp.concatenate([bh, bm, bh, bm, bl, bh], axis=dim_b)
    return matmul(left, right, dim_a, dim_b)


def on_chip(shape, dtype):
    return pltpu.VMEM(shape, dtype)


def in_hbm(*values):
    return [pltpu.with_memory_space_constraint(value, pltpu.HBM) for value in values]


def held(*values):
    return [pltpu.with_memory_space_constraint(value, pltpu.VMEM) for value in values]


def sketch_kernel(
    scale,
    steps,
    flag_ref,
    snap_ref,
    sketch_ref,
    out_ref,
    x1_ref,
    x2_ref,
    y1_ref,
    y2_ref,
    z1_ref,
    z2_ref,
    sent_ref,
    kept_ref,
    rows_ref,
    table_ref,
    parts_ref,
    gram_ref,
    sems,
):
    cells_x, cells_y, cells_z, columns = out_ref.shape
    half = columns // 2
    planes = cells_x // steps
    table = pltpu.make_async_copy(sketch_ref, table_ref, sems.at[steps])
    table.start()
    copies = []
    for i in range(steps):
        span = pl.ds(i * planes, planes)
        copies.append(pltpu.make_async_copy(snap_ref.at[span], rows_ref.at[span], sems.at[i]))
        copies[-1].start()
    table.wait()
    for i, part in enumerate(split3(table_ref[...])):
        parts_ref[i * columns : (i + 1) * columns, :] = part
    even = [flag_ref[k] == 0 for k in range(3)]
    for i in range(steps):
        copies[i].wait()
        span = slice(i * planes, (i + 1) * planes)
        rows = rows_ref[span].reshape(-1, columns)
        made = matmul(jnp.concatenate([rows, rows, rows], axis=1), parts_ref[...], 1, 0)
        made = made.astype(bf16)
        gram = matmul(made, made, 0, 0)
        for at, value in (
            (0, gram[:half, :half]),
            (half, gram[:half, half:]),
            (columns, gram[half:, half:]),
        ):
            value = value if i == 0 else gram_ref[at : at + half, :] + value
            gram_ref[at : at + half, :] = value * scale if i == steps - 1 else value
        out_ref[span] = made.reshape(planes, cells_y, cells_z, columns)
        field = out_ref[span]
        low_y, high_y = field[:, 0], field[:, cells_y - 1]
        y1_ref[span] = jnp.where(even[1], high_y, low_y)
        y2_ref[span] = jnp.where(even[1], low_y, high_y)
        low_z = field[:, :, 0, :].astype(f32)
        high_z = field[:, :, cells_z - 1, :].astype(f32)
        z1_ref[span] = jnp.where(even[2], high_z, low_z).astype(bf16)
        z2_ref[span] = jnp.where(even[2], low_z, high_z).astype(bf16)
    low_x, high_x = out_ref[0], out_ref[cells_x - 1]
    x1_ref[...] = jnp.where(even[0], high_x, low_x)
    x2_ref[...] = jnp.where(even[0], low_x, high_x)
    size = sent_ref.shape[0]
    mine = pl.multiple_of(flag_ref[3] * size, size)
    other = pl.multiple_of((1 - flag_ref[3]) * size, size)
    kept_ref[...] = gram_ref[pl.ds(mine, size), :]
    sent_ref[...] = gram_ref[pl.ds(other, size), :]


def sketch_call(flags, snapshots, sketch, scale):
    cells_x, cells_y, cells_z, columns = snapshots.shape
    half = columns // 2
    steps = 4
    return pl.pallas_call(
        functools.partial(sketch_kernel, scale, steps),
        in_specs=[SMEM, HBM, HBM],
        out_specs=[VMEM] * 9,
        out_shape=[
            on_chip(snapshots.shape, bf16),
            on_chip((cells_y, cells_z, columns), bf16),
            on_chip((cells_y, cells_z, columns), bf16),
            on_chip((cells_x, cells_z, columns), bf16),
            on_chip((cells_x, cells_z, columns), bf16),
            on_chip((cells_x, cells_y, columns), bf16),
            on_chip((cells_x, cells_y, columns), bf16),
            on_chip((3 * half // 2, half), f32),
            on_chip((3 * half // 2, half), f32),
        ],
        scratch_shapes=[
            pltpu.VMEM(snapshots.shape, bf16),
            pltpu.VMEM(sketch.shape, f32),
            pltpu.VMEM((3 * columns, columns), bf16),
            pltpu.VMEM((3 * half, half), f32),
            pltpu.SemaphoreType.DMA((steps + 1,)),
        ],
        compiler_params=PARAMS,
        name="sketch",
    )(flags, *in_hbm(snapshots, sketch))


def operator_kernel(
    scale,
    planes,
    flag_ref,
    s_ref,
    x1_ref,
    x2_ref,
    y1_ref,
    y2_ref,
    z1_ref,
    z2_ref,
    coef_ref,
    *refs,
):
    cells_x, cells_y, _, columns = s_ref.shape
    first = planes[0]
    even = [flag_ref[k] == 0 for k in range(3)]
    if first == 0:
        image_ref, total_ref = refs
    else:
        sum_ref, image_ref, sent_ref, kept_ref, total_ref = refs
    for x in planes:
        plane = s_ref[x]
        if x > 0:
            before = s_ref[x - 1]
        else:
            before = jnp.where(even[0], x2_ref[...], x1_ref[...])
        if x < cells_x - 1:
            after = s_ref[x + 1]
        else:
            after = jnp.where(even[0], x1_ref[...], x2_ref[...])
        before, after, middle = before.astype(f32), after.astype(f32), plane.astype(f32)
        y1, y2 = y1_ref[x].astype(f32), y2_ref[x].astype(f32)
        z1, z2 = z1_ref[x].astype(f32), z2_ref[x].astype(f32)
        south = jnp.concatenate([jnp.where(even[1], y2, y1)[None], middle[:-1]], axis=0)
        north = jnp.concatenate([middle[1:], jnp.where(even[1], y1, y2)[None]], axis=0)
        below = jnp.where(even[2], z2, z1)[:, None, :]
        above = jnp.where(even[2], z1, z2)[:, None, :]
        lower = jnp.concatenate([below, middle[:, :-1]], axis=1)
        upper = jnp.concatenate([middle[:, 1:], above], axis=1)
        around = (after + before) + (north + south) + (upper + lower)

        def spread(k):
            return jnp.stack([coef_ref[k, x, :, y : y + 1] for y in range(cells_y)], axis=0)

        image = spread(3) * (6.0 * middle - around)
        image = image + spread(0) * (after - before)
        image = image + spread(1) * (north - south)
        image = image + spread(2) * (upper - lower)
        high, low = split2(image.reshape(-1, columns))
        count = high.shape[0]
        at = (x - first) * count
        image_ref[at : at + count, :columns] = high
        image_ref[at : at + count, columns:] = low
        base = plane.reshape(-1, columns)
        part = matmul(
            jnp.concatenate([base, base], axis=0), jnp.concatenate([high, low], axis=0), 0, 0
        )
        if x > first:
            part = total_ref[...] + part
        elif first > 0:
            part = sum_ref[...] + part
        if x < cells_x - 1:
            total_ref[...] = part
        else:
            total_ref[...] = part * scale
            size = columns // 2
            mine = pl.multiple_of(flag_ref[3] * size, size)
            other = pl.multiple_of((1 - flag_ref[3]) * size, size)
            for at in (0, size):
                kept_ref[at : at + size, :] = total_ref[pl.ds(mine, size), at : at + size]
                sent_ref[at : at + size, :] = total_ref[pl.ds(other, size), at : at + size]


def operator_calls(flags, sketched, halos, coefs, scale):
    cells_x, cells_y, cells_z, columns = sketched.shape
    half = cells_x // 2
    image = on_chip((half * cells_y * cells_z, 2 * columns), bf16)
    image0, partial = pl.pallas_call(
        functools.partial(operator_kernel, scale, range(half)),
        in_specs=[SMEM] + [VMEM] * 8,
        out_specs=[VMEM] * 2,
        out_shape=[image, on_chip((columns, columns), f32)],
        compiler_params=PARAMS,
        name="operator0",
    )(flags, *held(sketched, *halos, coefs))
    image1, sent, kept = pl.pallas_call(
        functools.partial(operator_kernel, scale, range(half, cells_x)),
        in_specs=[SMEM] + [VMEM] * 9,
        out_specs=[VMEM] * 3,
        out_shape=[image] + [on_chip((columns, columns // 2), f32)] * 2,
        scratch_shapes=[pltpu.VMEM((columns, columns), f32)],
        compiler_params=PARAMS,
        name="operator1",
    )(flags, *held(sketched, *halos, coefs, partial))
    return image0, image1, sent, kept


def eliminate(block):
    size = block.shape[0]
    sub = lax.broadcasted_iota(jnp.int32, (TILE, size), 0)
    lane = lax.broadcasted_iota(jnp.int32, (TILE, size), 1)
    tiles = [block[i : i + TILE, :] for i in range(0, size, TILE)]
    count = size // TILE
    pivots = []

    def full(value):
        return jnp.broadcast_to(value, (TILE, size))

    for s in range(count):
        at = s * TILE
        tile = tiles[s]
        cols = [
            [full(tiles[t][:, at + k : at + k + 1]) for k in range(TILE)] for t in range(s, count)
        ]
        a = [[full(cols[0][k][i : i + 1, :]) for k in range(i + 1)] for i in range(TILE)]
        w = [[None] * TILE for _ in range(TILE)]
        r = []
        for j in range(TILE):
            r.append(1.0 / a[j][j])
            m = [a[i][j] * r[j] if i > j else None for i in range(TILE)]
            for i in range(j + 1, TILE):
                for k in range(j + 1, i + 1):
                    a[i][k] = a[i][k] - m[i] * a[k][j]
                for k in range(j):
                    w[i][k] = w[i][k] - m[i] * w[j][k]
                w[i][j] = -m[i]
        unit = []
        for k in range(TILE):
            col = jnp.where(sub == k, 1.0, 0.0)
            for i in range(k + 1, TILE):
                col = jnp.where(sub == i, w[i][k], col)
            unit.append(col)
        pivot = r[0]
        for i in range(1, TILE):
            pivot = jnp.where(sub == i, r[i], pivot)
        pivots.append(pivot[:, :1])
        new = unit[0] * full(tile[:1, :])
        for k in range(1, TILE):
            new = new + unit[k] * full(tile[k : k + 1, :])
        for k in range(TILE):
            new = jnp.where(lane == at + k, unit[k], new)
        tiles[s] = new
        if s == count - 1:
            break
        rows = [full(new[k : k + 1, :]) for k in range(TILE)]
        inside = (lane >= at) & (lane < at + TILE)
        for t in range(s + 1, count):
            col = cols[t - s]
            left = jnp.where(inside, 0.0, tiles[t])
            for k in range(TILE):
                factor = col[k]
                for i in range(k):
                    factor = factor + w[k][i] * col[i]
                left = left - (factor * r[k]) * rows[k]
            tiles[t] = left
    result = jnp.concatenate(tiles, axis=0)
    row_b = lax.broadcasted_iota(jnp.int32, (size, size), 0)
    lane_b = lax.broadcasted_iota(jnp.int32, (size, size), 1)
    return jnp.where(lane_b <= row_b, result, 0.0), jnp.concatenate(pivots, axis=0)


def factor_kernel(start, *refs):
    if start == 0:
        flag_ref, part_ref, other_ref, out_ref, next_ref, state_ref = refs
        half = state_ref.shape[1] // 2
        own_first = flag_ref[3] == 0
        part, other = part_ref[...], other_ref[...]
        upper = jnp.where(own_first, part, other)
        under = jnp.where(own_first, other, part)
        both = jnp.concatenate([upper, under], axis=0)
        state_ref[:half, :half] = both[:half]
        state_ref[:half, half:] = both[half : 2 * half]
        state_ref[half:, :half] = jnp.zeros((half, half), f32)
        state_ref[half:, half:] = both[2 * half :]
    elif len(refs) == 3:
        state_ref, out_ref, next_ref = refs
    else:
        state_ref, out_ref = refs
        next_ref = None
    n = state_ref.shape[1]
    end = start + PANEL
    lane = lax.broadcasted_iota(jnp.int32, (PANEL, n), 1)
    unit, pivots = eliminate(state_ref[:PANEL, start:end])
    panel = dot_f32(unit, state_ref[:PANEL, :], 1, 0)
    pieces = [unit]
    if start:
        pieces = [jnp.zeros((PANEL, start), f32)] + pieces
    if end < n:
        pieces = pieces + [jnp.zeros((PANEL, n - end), f32)]
    inside = (lane >= start) & (lane < end)
    rows = jnp.where(inside, jnp.concatenate(pieces, axis=1), panel)
    out_ref[...] = jnp.where(lane < end, rows * jnp.sqrt(pivots), 0.0)
    if end < n:
        factors = (panel * pivots)[:, end:]
        lane_r = lax.broadcasted_iota(jnp.int32, (n - end, n), 1)
        old = jnp.where((lane_r >= start) & (lane_r < end), 0.0, state_ref[PANEL:, :])
        next_ref[...] = old - dot_f32(factors, rows, 0, 0)


def factor_calls(flags, part, other):
    n = part.shape[1] * 2
    rows = []
    state = None
    for start in range(0, n, PANEL):
        left = n - start - PANEL
        outs = [on_chip((PANEL, n), f32)]
        if left:
            outs.append(on_chip((left, n), f32))
        args = (flags, *held(part, other)) if start == 0 else held(state)
        got = pl.pallas_call(
            functools.partial(factor_kernel, start),
            in_specs=[SMEM, VMEM, VMEM] if start == 0 else [VMEM],
            out_specs=[VMEM] * len(outs),
            out_shape=outs,
            scratch_shapes=[pltpu.VMEM((n, n), f32)] if start == 0 else [],
            compiler_params=PARAMS,
        )(*args)
        rows.append(got[0])
        if left:
            state = got[1]
    return rows


def finish_kernel(steps, flag_ref, part_ref, other_ref, image0_ref, image1_ref, *refs):
    count = len(refs) - 5
    inverse_refs, (out_ref, reduced_ref, right_ref, made_ref, sems) = refs[:count], refs[count:]
    columns = out_ref.shape[1]
    half = columns // 2
    inverse = jnp.concatenate([ref[...] for ref in inverse_refs], axis=0)
    own_first = flag_ref[3] == 0
    part = jnp.concatenate([part_ref[:half, :], part_ref[half:, :]], axis=1)
    other = jnp.concatenate([other_ref[:half, :], other_ref[half:, :]], axis=1)
    gram = jnp.concatenate(
        [jnp.where(own_first, part, other), jnp.where(own_first, other, part)], axis=0
    )
    high, low = split2(inverse)
    right_ref[...] = jnp.concatenate([high, low, high], axis=1)
    right = right_ref[...]
    block = out_ref.shape[0] // steps
    copies = []

    def applied(i):
        ref, at = (image0_ref, i) if i < steps // 2 else (image1_ref, i - steps // 2)
        image = ref[at * block : (at + 1) * block, :]
        left = jnp.concatenate([image[:, :columns], image], axis=1)
        span = pl.ds(i * block, block)
        made_ref[span, :] = matmul(left, right, 1, 1).astype(bf16)
        copies.append(pltpu.make_async_copy(made_ref.at[span], out_ref.at[span], sems.at[i]))
        copies[-1].start()

    middle = dot_f32(inverse, gram, 1, 0)
    for i in range(steps - 1):
        applied(i)
    reduced_ref[...] = dot_f32(middle, inverse, 1, 1)
    applied(steps - 1)
    for copy in copies:
        copy.wait()


def finish_call(flags, part, other, image0, image1, rows):
    count, columns = image0.shape[0] * 2, image0.shape[1] // 2
    steps = 4
    return pl.pallas_call(
        functools.partial(finish_kernel, steps),
        in_specs=[SMEM] + [VMEM] * (4 + len(rows)),
        out_specs=[HBM, VMEM],
        out_shape=[
            jax.ShapeDtypeStruct((count, columns), bf16),
            jax.ShapeDtypeStruct((columns, columns), f32),
        ],
        scratch_shapes=[
            pltpu.VMEM((columns, 3 * columns), bf16),
            pltpu.VMEM((count, columns), bf16),
            pltpu.SemaphoreType.DMA((steps,)),
        ],
        compiler_params=PARAMS,
        name="finish",
    )(flags, *held(part, other, image0, image1, *rows))


AXES = ("gx", "gy", "gz")
PLANE = ("gx", "gy")


def swap(value, masks):
    depth = lax.axis_size("gz")
    pairs = [(i, i ^ masks[i // depth % 2]) for i in range(lax.axis_size(AXES))]
    return lax.ppermute(value, AXES, pairs)


def stages():
    depth = lax.axis_size("gz")
    plane, line = [], []
    mask = 2
    while mask < lax.axis_size(PLANE):
        plane.append(mask * depth)
        mask *= 2
    mask = 1
    while mask < depth:
        line.append(mask)
        mask *= 2
    bits = line[-1:] + plane + line[:-1]
    turned = list(bits)
    for k in range(0, len(bits) - 1, 2):
        turned[k], turned[k + 1] = bits[k + 1], bits[k]
    return list(zip(bits, turned))


def exchange(part, masks):
    got = swap(part, masks)
    return part + got


def trade(sent):
    depth = lax.axis_size("gz")
    return swap(sent, (depth, depth))


def halo_pair(first, second, axis):
    count = lax.axis_size(axis)
    got = []
    for start, layer in ((0, first), (1, second)):
        pairs = []
        for i in range(start, count - 1, 2):
            pairs += [(i, i + 1), (i + 1, i)]
        if pairs:
            got.append(lax.ppermute(layer, axis, pairs))
        else:
            got.append(jnp.zeros_like(layer))
    return got


def body(snapshots, sketch, velocity, viscosity):
    shape = snapshots.shape
    ncells = shape[0] * shape[1] * shape[2]
    for axis in ("gx", "gy", "gz"):
        ncells *= lax.axis_size(axis)
    scale = 1.0 / ncells
    flags = [lax.axis_index(axis) % 2 for axis in ("gx", "gy", "gz")]
    flags = jnp.stack(flags + [lax.axis_index(PLANE) % 2]).astype(jnp.int32)
    coefs = jnp.concatenate([0.5 * velocity, viscosity[None]], axis=0).transpose(0, 1, 3, 2)
    sketched, x1, x2, y1, y2, z1, z2, sent, kept = sketch_call(
        flags, snapshots, sketch, scale
    )
    steps = stages()
    ahead = min(2, len(steps))
    part = kept + trade(sent)
    for k in range(ahead):
        part = exchange(part, steps[k])
    halos = halo_pair(x1, x2, "gx") + halo_pair(y1, y2, "gy")
    halos = halos + halo_pair(z1, z2, "gz")
    image0, image1, sent, kept = operator_calls(flags, sketched, halos, coefs, scale)
    i_part = kept + trade(sent)
    size = part.shape[0]
    both = jnp.concatenate([part, i_part], axis=0)
    for k in range(ahead, len(steps)):
        both = exchange(both, steps[k])
    part, i_part = both[:size], both[size:]
    other = trade(part)
    rows = factor_calls(flags, part, other)
    for k in range(ahead):
        i_part = exchange(i_part, steps[k])
    i_other = trade(i_part)
    applied, reduced = finish_call(flags, i_part, i_other, image0, image1, rows)
    return applied.reshape(shape), reduced


def solution(mesh):
    in_specs = (P("gx", "gy", "gz", None), P(), P(None, "gx", "gy", "gz"), P("gx", "gy", "gz"))
    out_specs = (P("gx", "gy", "gz", None), P())
    return jax.shard_map(body, mesh=mesh, in_specs=in_specs, out_specs=out_specs, check_vma=False)
```

```python
import functools

import jax
import jax.numpy as jnp
from jax import lax
from jax.experimental import pallas as pl
from jax.experimental.pallas import tpu as pltpu
from jax.sharding import PartitionSpec as P

f32 = jnp.float32
bf16 = jnp.bfloat16
VMEM = pl.BlockSpec(memory_space=pltpu.VMEM)
SMEM = pl.BlockSpec(memory_space=pltpu.SMEM)
HBM = pl.BlockSpec(memory_space=pltpu.HBM)
PARAMS = pltpu.CompilerParams(vmem_limit_bytes=16 << 20)
TILE = 8
PANEL = 64


def split2(x):
    high = x.astype(bf16)
    return high, (x - high.astype(f32)).astype(bf16)


def split3(x):
    high = x.astype(bf16)
    return (high, *split2(x - high.astype(f32)))


def matmul(a, b, dim_a, dim_b):
    return lax.dot_general(a, b, (((dim_a,), (dim_b,)), ((), ())), preferred_element_type=f32)


def dot_f32(a, b, dim_a, dim_b):
    ah, am, al = split3(a)
    bh, bm, bl = split3(b)
    left = jnp.concatenate([ah, ah, am, am, ah, al], axis=dim_a)
    right = jnp.concatenate([bh, bm, bh, bm, bl, bh], axis=dim_b)
    return matmul(left, right, dim_a, dim_b)


def on_chip(shape, dtype):
    return pltpu.VMEM(shape, dtype)


def in_hbm(*values):
    return [pltpu.with_memory_space_constraint(value, pltpu.HBM) for value in values]


def held(*values):
    return [pltpu.with_memory_space_constraint(value, pltpu.VMEM) for value in values]


def sketch_kernel(
    scale,
    steps,
    flag_ref,
    snap_ref,
    sketch_ref,
    velocity_ref,
    viscosity_ref,
    out_ref,
    x1_ref,
    x2_ref,
    y1_ref,
    y2_ref,
    z1_ref,
    z2_ref,
    sent_ref,
    kept_ref,
    coef_ref,
    rows_ref,
    table_ref,
    parts_ref,
    gram_ref,
    flow_ref,
    sems,
):
    cells_x, cells_y, cells_z, columns = out_ref.shape
    half = columns // 2
    planes = cells_x // steps
    table = pltpu.make_async_copy(sketch_ref, table_ref, sems.at[steps])
    table.start()
    copies = []
    for i in range(steps):
        span = pl.ds(i * planes, planes)
        copies.append(pltpu.make_async_copy(snap_ref.at[span], rows_ref.at[span], sems.at[i]))
        copies[-1].start()
    flow = pltpu.make_async_copy(velocity_ref, flow_ref.at[:3], sems.at[steps + 1])
    flow.start()
    spread = pltpu.make_async_copy(viscosity_ref, flow_ref.at[3], sems.at[steps + 2])
    spread.start()
    table.wait()
    for i, part in enumerate(split3(table_ref[...])):
        parts_ref[i * columns : (i + 1) * columns, :] = part
    even = [flag_ref[k] == 0 for k in range(3)]
    for i in range(steps):
        copies[i].wait()
        span = slice(i * planes, (i + 1) * planes)
        rows = rows_ref[span].reshape(-1, columns)
        made = matmul(jnp.concatenate([rows, rows, rows], axis=1), parts_ref[...], 1, 0)
        made = made.astype(bf16)
        gram = matmul(made, made, 0, 0)
        for at, value in (
            (0, gram[:half, :half]),
            (half, gram[:half, half:]),
            (columns, gram[half:, half:]),
        ):
            value = value if i == 0 else gram_ref[at : at + half, :] + value
            gram_ref[at : at + half, :] = value * scale if i == steps - 1 else value
        out_ref[span] = made.reshape(planes, cells_y, cells_z, columns)
        field = out_ref[span]
        low_y, high_y = field[:, 0], field[:, cells_y - 1]
        y1_ref[span] = jnp.where(even[1], high_y, low_y)
        y2_ref[span] = jnp.where(even[1], low_y, high_y)
        low_z = field[:, :, 0, :].astype(f32)
        high_z = field[:, :, cells_z - 1, :].astype(f32)
        z1_ref[span] = jnp.where(even[2], high_z, low_z).astype(bf16)
        z2_ref[span] = jnp.where(even[2], low_z, high_z).astype(bf16)
    flow.wait()
    spread.wait()
    for k in range(4):
        for x in range(cells_x):
            plane = flow_ref[k, x].T
            coef_ref[k, x] = 0.5 * plane if k < 3 else plane
    low_x, high_x = out_ref[0], out_ref[cells_x - 1]
    x1_ref[...] = jnp.where(even[0], high_x, low_x)
    x2_ref[...] = jnp.where(even[0], low_x, high_x)
    size = sent_ref.shape[0]
    mine = pl.multiple_of(flag_ref[3] * size, size)
    other = pl.multiple_of((1 - flag_ref[3]) * size, size)
    kept_ref[...] = gram_ref[pl.ds(mine, size), :]
    sent_ref[...] = gram_ref[pl.ds(other, size), :]


def sketch_call(flags, snapshots, sketch, velocity, viscosity, scale):
    cells_x, cells_y, cells_z, columns = snapshots.shape
    half = columns // 2
    steps = 2
    return pl.pallas_call(
        functools.partial(sketch_kernel, scale, steps),
        in_specs=[SMEM] + [HBM] * 4,
        out_specs=[VMEM] * 10,
        out_shape=[
            on_chip(snapshots.shape, bf16),
            on_chip((cells_y, cells_z, columns), bf16),
            on_chip((cells_y, cells_z, columns), bf16),
            on_chip((cells_x, cells_z, columns), bf16),
            on_chip((cells_x, cells_z, columns), bf16),
            on_chip((cells_x, cells_y, columns), bf16),
            on_chip((cells_x, cells_y, columns), bf16),
            on_chip((3 * half // 2, half), f32),
            on_chip((3 * half // 2, half), f32),
            on_chip((4, cells_x, cells_z, cells_y), f32),
        ],
        scratch_shapes=[
            pltpu.VMEM(snapshots.shape, bf16),
            pltpu.VMEM(sketch.shape, f32),
            pltpu.VMEM((3 * columns, columns), bf16),
            pltpu.VMEM((3 * half, half), f32),
            pltpu.VMEM((4, cells_x, cells_y, cells_z), f32),
            pltpu.SemaphoreType.DMA((steps + 3,)),
        ],
        compiler_params=PARAMS,
        name="sketch",
    )(flags, *in_hbm(snapshots, sketch, velocity, viscosity))


def operator_kernel(
    scale,
    planes,
    flag_ref,
    s_ref,
    x1_ref,
    x2_ref,
    y1_ref,
    y2_ref,
    z1_ref,
    z2_ref,
    coef_ref,
    *refs,
):
    cells_x, cells_y, cells_z, columns = s_ref.shape
    first = planes[0]
    even = [flag_ref[k] == 0 for k in range(3)]
    if first == 0:
        image_ref, total_ref = refs
    else:
        sum_ref, image_ref, sent_ref, kept_ref, total_ref = refs
    for x in planes:
        for y in range(cells_y):
            middle = s_ref[x, y].astype(f32)
            if x > 0:
                before = s_ref[x - 1, y]
            else:
                before = jnp.where(even[0], x2_ref[y], x1_ref[y])
            if x < cells_x - 1:
                after = s_ref[x + 1, y]
            else:
                after = jnp.where(even[0], x1_ref[y], x2_ref[y])
            before, after = before.astype(f32), after.astype(f32)
            if y > 0:
                south = s_ref[x, y - 1]
            else:
                south = jnp.where(even[1], y2_ref[x], y1_ref[x])
            if y < cells_y - 1:
                north = s_ref[x, y + 1]
            else:
                north = jnp.where(even[1], y1_ref[x], y2_ref[x])
            south, north = south.astype(f32), north.astype(f32)
            z1, z2 = z1_ref[x, y : y + 1].astype(f32), z2_ref[x, y : y + 1].astype(f32)
            below, above = jnp.where(even[2], z2, z1), jnp.where(even[2], z1, z2)
            lower = jnp.concatenate([below, middle[:-1]], axis=0)
            upper = jnp.concatenate([middle[1:], above], axis=0)
            around = (after + before) + (north + south) + (upper + lower)

            def spread(k):
                return jnp.broadcast_to(coef_ref[k, x, :, y : y + 1], middle.shape)

            image = spread(3) * (6.0 * middle - around)
            image = image + spread(0) * (after - before)
            image = image + spread(1) * (north - south)
            image = image + spread(2) * (upper - lower)
            high, low = split2(image)
            at = ((x - first) * cells_y + y) * cells_z
            image_ref[at : at + cells_z, :columns] = high
            image_ref[at : at + cells_z, columns:] = low
        plane = s_ref[x]
        at = (x - first) * cells_y * cells_z
        high = image_ref[at : at + cells_y * cells_z, :columns]
        low = image_ref[at : at + cells_y * cells_z, columns:]
        base = plane.reshape(-1, columns)
        part = matmul(
            jnp.concatenate([base, base], axis=0), jnp.concatenate([high, low], axis=0), 0, 0
        )
        if x > first:
            part = total_ref[...] + part
        elif first > 0:
            part = sum_ref[...] + part
        if x < cells_x - 1:
            total_ref[...] = part
        else:
            total_ref[...] = part * scale
            size = columns // 2
            mine = pl.multiple_of(flag_ref[3] * size, size)
            other = pl.multiple_of((1 - flag_ref[3]) * size, size)
            for at in (0, size):
                kept_ref[at : at + size, :] = total_ref[pl.ds(mine, size), at : at + size]
                sent_ref[at : at + size, :] = total_ref[pl.ds(other, size), at : at + size]


def operator_calls(flags, sketched, halos, coefs, scale):
    cells_x, cells_y, cells_z, columns = sketched.shape
    half = cells_x // 2
    image = on_chip((half * cells_y * cells_z, 2 * columns), bf16)
    image0, partial = pl.pallas_call(
        functools.partial(operator_kernel, scale, range(half)),
        in_specs=[SMEM] + [VMEM] * 8,
        out_specs=[VMEM] * 2,
        out_shape=[image, on_chip((columns, columns), f32)],
        compiler_params=PARAMS,
        name="operator0",
    )(flags, *held(sketched, *halos, coefs))
    image1, sent, kept = pl.pallas_call(
        functools.partial(operator_kernel, scale, range(half, cells_x)),
        in_specs=[SMEM] + [VMEM] * 9,
        out_specs=[VMEM] * 3,
        out_shape=[image] + [on_chip((columns, columns // 2), f32)] * 2,
        scratch_shapes=[pltpu.VMEM((columns, columns), f32)],
        compiler_params=PARAMS,
        name="operator1",
    )(flags, *held(sketched, *halos, coefs, partial))
    return image0, image1, sent, kept


def total(values):
    values = list(values)
    while len(values) > 1:
        pairs = zip(values[::2], values[1::2])
        values = [a + b for a, b in pairs] + values[len(values) // 2 * 2 :]
    return values[0]


def eliminate(block, cells_ref):
    size = block.shape[0]
    sub = lax.broadcasted_iota(jnp.int32, (TILE, size), 0)
    lane = lax.broadcasted_iota(jnp.int32, (TILE, size), 1)
    tiles = [block[i : i + TILE, :] for i in range(0, size, TILE)]
    count = size // TILE
    pivots = []

    def full(value):
        return jnp.broadcast_to(value, (TILE, size))

    for s in range(count):
        at = s * TILE
        tile = tiles[s]
        cols = [
            [full(tiles[t][:, at + k : at + k + 1]) for k in range(TILE)] for t in range(s, count)
        ]
        for k in range(TILE):
            cells_ref[k * TILE : (k + 1) * TILE, :] = cols[0][k]
        a = [
            [cells_ref[pl.ds(k * TILE + i, TILE, stride=0), :] for k in range(i + 1)]
            for i in range(TILE)
        ]
        w = [[None] * TILE for _ in range(TILE)]
        r = []
        for j in range(TILE):
            r.append(1.0 / a[j][j])
            m = [a[i][j] * r[j] if i > j else None for i in range(TILE)]
            for i in range(j + 1, TILE):
                for k in range(j + 1, i + 1):
                    a[i][k] = a[i][k] - m[i] * a[k][j]
                for k in range(j):
                    w[i][k] = w[i][k] - m[i] * w[j][k]
                w[i][j] = -m[i]
        unit = []
        for k in range(TILE):
            col = jnp.where(sub == k, 1.0, 0.0)
            for i in range(k + 1, TILE):
                col = jnp.where(sub == i, w[i][k], col)
            unit.append(col)
        pivot = r[0]
        for i in range(1, TILE):
            pivot = jnp.where(sub == i, r[i], pivot)
        pivots.append(pivot[:, :1])
        new = total(unit[k] * full(tile[k : k + 1, :]) for k in range(TILE))
        for k in range(TILE):
            new = jnp.where(lane == at + k, unit[k], new)
        tiles[s] = new
        if s == count - 1:
            break
        rows = [full(new[k : k + 1, :]) * r[k] for k in range(TILE)]
        inside = (lane >= at) & (lane < at + TILE)
        for t in range(s + 1, count):
            col = cols[t - s]
            terms = []
            for k in range(TILE):
                factor = total([col[k]] + [w[k][i] * col[i] for i in range(k)])
                terms.append(factor * rows[k])
            tiles[t] = jnp.where(inside, 0.0, tiles[t]) - total(terms)
    result = jnp.concatenate(tiles, axis=0)
    row_b = lax.broadcasted_iota(jnp.int32, (size, size), 0)
    lane_b = lax.broadcasted_iota(jnp.int32, (size, size), 1)
    return jnp.where(lane_b <= row_b, result, 0.0), jnp.concatenate(pivots, axis=0)


def factor_kernel(start, *refs):
    refs, cells_ref = refs[:-1], refs[-1]
    if start == 0:
        flag_ref, part_ref, other_ref, out_ref, next_ref, state_ref = refs
        half = state_ref.shape[1] // 2
        own_first = flag_ref[3] == 0
        part, other = part_ref[...], other_ref[...]
        upper = jnp.where(own_first, part, other)
        under = jnp.where(own_first, other, part)
        both = jnp.concatenate([upper, under], axis=0)
        state_ref[:half, :half] = both[:half]
        state_ref[:half, half:] = both[half : 2 * half]
        state_ref[half:, :half] = jnp.zeros((half, half), f32)
        state_ref[half:, half:] = both[2 * half :]
    elif len(refs) == 3:
        state_ref, out_ref, next_ref = refs
    else:
        state_ref, out_ref = refs
        next_ref = None
    n = state_ref.shape[1]
    end = start + PANEL
    lane = lax.broadcasted_iota(jnp.int32, (PANEL, n), 1)
    unit, pivots = eliminate(state_ref[:PANEL, start:end], cells_ref)
    panel = dot_f32(unit, state_ref[:PANEL, :], 1, 0)
    pieces = [unit]
    if start:
        pieces = [jnp.zeros((PANEL, start), f32)] + pieces
    if end < n:
        pieces = pieces + [jnp.zeros((PANEL, n - end), f32)]
    inside = (lane >= start) & (lane < end)
    rows = jnp.where(inside, jnp.concatenate(pieces, axis=1), panel)
    out_ref[...] = jnp.where(lane < end, rows * jnp.sqrt(pivots), 0.0)
    if end < n:
        factors = (panel * pivots)[:, end:]
        lane_r = lax.broadcasted_iota(jnp.int32, (n - end, n), 1)
        old = jnp.where((lane_r >= start) & (lane_r < end), 0.0, state_ref[PANEL:, :])
        next_ref[...] = old - dot_f32(factors, rows, 0, 0)


def factor_calls(flags, part, other):
    n = part.shape[1] * 2
    rows = []
    state = None
    for start in range(0, n, PANEL):
        left = n - start - PANEL
        outs = [on_chip((PANEL, n), f32)]
        if left:
            outs.append(on_chip((left, n), f32))
        args = (flags, *held(part, other)) if start == 0 else held(state)
        got = pl.pallas_call(
            functools.partial(factor_kernel, start),
            in_specs=[SMEM, VMEM, VMEM] if start == 0 else [VMEM],
            out_specs=[VMEM] * len(outs),
            out_shape=outs,
            scratch_shapes=([pltpu.VMEM((n, n), f32)] if start == 0 else [])
            + [pltpu.VMEM((TILE * TILE, PANEL), f32)],
            compiler_params=PARAMS,
        )(*args)
        rows.append(got[0])
        if left:
            state = got[1]
    return rows


def finish_kernel(steps, flag_ref, part_ref, other_ref, image0_ref, image1_ref, *refs):
    count = len(refs) - 6
    inverse_refs, rest = refs[:count], refs[count:]
    out_ref, reduced_ref, right_ref, made_ref, sum_ref, sems = rest
    columns = out_ref.shape[1]
    half = columns // 2
    inverse = jnp.concatenate([ref[...] for ref in inverse_refs], axis=0)
    own_first = flag_ref[3] == 0
    part = jnp.concatenate([part_ref[:half, :], part_ref[half:, :]], axis=1)
    other = jnp.concatenate([other_ref[:half, :], other_ref[half:, :]], axis=1)
    gram = jnp.concatenate(
        [jnp.where(own_first, part, other), jnp.where(own_first, other, part)], axis=0
    )
    high, low = split2(inverse)
    right_ref[...] = jnp.concatenate([high, low, high], axis=1)
    right = right_ref[...]
    block = out_ref.shape[0] // steps
    copies = []

    def send(source, target):
        copies.append(pltpu.make_async_copy(source, target, sems.at[len(copies)]))
        copies[-1].start()

    def applied(i):
        ref, at = (image0_ref, i) if i < steps // 2 else (image1_ref, i - steps // 2)
        image = ref[at * block : (at + 1) * block, :]
        left = jnp.concatenate([image[:, :columns], image], axis=1)
        made_ref[i * block : (i + 1) * block, :] = matmul(left, right, 1, 1).astype(bf16)

    middle = dot_f32(inverse, gram, 1, 0)
    for i in range(steps - 1):
        applied(i)
    span = pl.ds(0, (steps - 1) * block)
    send(made_ref.at[span], out_ref.at[span])
    sum_ref[...] = dot_f32(middle, inverse, 1, 1)
    applied(steps - 1)
    span = pl.ds((steps - 1) * block, block)
    send(sum_ref, reduced_ref)
    send(made_ref.at[span], out_ref.at[span])
    for copy in copies:
        copy.wait()


def finish_call(flags, part, other, image0, image1, rows):
    count, columns = image0.shape[0] * 2, image0.shape[1] // 2
    steps = 4
    return pl.pallas_call(
        functools.partial(finish_kernel, steps),
        in_specs=[SMEM] + [VMEM] * (4 + len(rows)),
        out_specs=[HBM, HBM],
        out_shape=[
            jax.ShapeDtypeStruct((count, columns), bf16),
            jax.ShapeDtypeStruct((columns, columns), f32),
        ],
        scratch_shapes=[
            pltpu.VMEM((columns, 3 * columns), bf16),
            pltpu.VMEM((count, columns), bf16),
            pltpu.VMEM((columns, columns), f32),
            pltpu.SemaphoreType.DMA((3,)),
        ],
        compiler_params=PARAMS,
        name="finish",
    )(flags, *held(part, other, image0, image1, *rows))


AXES = ("gx", "gy", "gz")
PLANE = ("gx", "gy")


def swap(value, masks):
    depth = lax.axis_size("gz")
    pairs = [(i, i ^ masks[i // depth % 2]) for i in range(lax.axis_size(AXES))]
    return lax.ppermute(value, AXES, pairs)


def stages():
    depth = lax.axis_size("gz")
    plane, line = [], []
    mask = 2
    while mask < lax.axis_size(PLANE):
        plane.append(mask * depth)
        mask *= 2
    mask = 1
    while mask < depth:
        line.append(mask)
        mask *= 2
    bits = line[-1:] + plane + line[:-1]
    turned = list(bits)
    for k in range(0, len(bits) - 1, 2):
        turned[k], turned[k + 1] = bits[k + 1], bits[k]
    return list(zip(bits, turned))


def exchange(part, masks):
    got = swap(part, masks)
    return part + got


def trade(sent):
    depth = lax.axis_size("gz")
    return swap(sent, (depth, depth))


def halo_pair(first, second, axis):
    count = lax.axis_size(axis)
    got = []
    for start, layer in ((0, first), (1, second)):
        pairs = []
        for i in range(start, count - 1, 2):
            pairs += [(i, i + 1), (i + 1, i)]
        if pairs:
            got.append(lax.ppermute(layer, axis, pairs))
        else:
            got.append(jnp.zeros_like(layer))
    return got


def body(snapshots, sketch, velocity, viscosity):
    shape = snapshots.shape
    ncells = shape[0] * shape[1] * shape[2]
    for axis in ("gx", "gy", "gz"):
        ncells *= lax.axis_size(axis)
    scale = 1.0 / ncells
    flags = [lax.axis_index(axis) % 2 for axis in ("gx", "gy", "gz")]
    flags = jnp.stack(flags + [lax.axis_index(PLANE) % 2]).astype(jnp.int32)
    sketched, x1, x2, y1, y2, z1, z2, sent, kept, coefs = sketch_call(
        flags, snapshots, sketch, velocity, viscosity, scale
    )
    steps = stages()
    part = kept + trade(sent)
    for masks in steps:
        part = exchange(part, masks)
    other = trade(part)
    halos = halo_pair(x1, x2, "gx") + halo_pair(y1, y2, "gy")
    halos = halos + halo_pair(z1, z2, "gz")
    image0, image1, sent, kept = operator_calls(flags, sketched, halos, coefs, scale)
    i_part = kept + trade(sent)
    turn = [3, 0, 1, 2] if len(steps) == 4 else range(len(steps))
    for stage in turn:
        i_part = exchange(i_part, steps[stage])
    i_other = trade(i_part)
    rows = factor_calls(flags, part, other)
    applied, reduced = finish_call(flags, i_part, i_other, image0, image1, rows)
    return applied.reshape(shape), reduced


def solution(mesh):
    in_specs = (P("gx", "gy", "gz", None), P(), P(None, "gx", "gy", "gz"), P("gx", "gy", "gz"))
    out_specs = (P("gx", "gy", "gz", None), P())
    return jax.shard_map(body, mesh=mesh, in_specs=in_specs, out_specs=out_specs, check_vma=False)
```

```python
import functools

import jax
import jax.numpy as jnp
from jax import lax
from jax.experimental import pallas as pl
from jax.experimental.pallas import tpu as pltpu
from jax.sharding import PartitionSpec as P

f32 = jnp.float32
bf16 = jnp.bfloat16
VMEM = pl.BlockSpec(memory_space=pltpu.VMEM)
SMEM = pl.BlockSpec(memory_space=pltpu.SMEM)
HBM = pl.BlockSpec(memory_space=pltpu.HBM)
PARAMS = pltpu.CompilerParams(vmem_limit_bytes=16 << 20)
TILE = 8
PANEL = 64


def split2(x):
    high = x.astype(bf16)
    return high, (x - high.astype(f32)).astype(bf16)


def split3(x):
    high = x.astype(bf16)
    return (high, *split2(x - high.astype(f32)))


def matmul(a, b, dim_a, dim_b):
    return lax.dot_general(a, b, (((dim_a,), (dim_b,)), ((), ())), preferred_element_type=f32)


def dot_f32(a, b, dim_a, dim_b):
    ah, am, al = split3(a)
    bh, bm, bl = split3(b)
    left = jnp.concatenate([ah, ah, am, am, ah, al], axis=dim_a)
    right = jnp.concatenate([bh, bm, bh, bm, bl, bh], axis=dim_b)
    return matmul(left, right, dim_a, dim_b)


def on_chip(shape, dtype):
    return pltpu.VMEM(shape, dtype)


def in_hbm(*values):
    return [pltpu.with_memory_space_constraint(value, pltpu.HBM) for value in values]


def held(*values):
    return [pltpu.with_memory_space_constraint(value, pltpu.VMEM) for value in values]


def sketch_kernel(
    scale,
    steps,
    flag_ref,
    snap_ref,
    sketch_ref,
    velocity_ref,
    viscosity_ref,
    out_ref,
    x1_ref,
    x2_ref,
    y1_ref,
    y2_ref,
    z1_ref,
    z2_ref,
    sent_ref,
    kept_ref,
    coef_ref,
    rows_ref,
    table_ref,
    parts_ref,
    gram_ref,
    flow_ref,
    sems,
):
    cells_x, cells_y, cells_z, columns = out_ref.shape
    half = columns // 2
    planes = cells_x // steps
    table = pltpu.make_async_copy(sketch_ref, table_ref, sems.at[steps])
    table.start()
    copies = []
    for i in range(steps):
        span = pl.ds(i * planes, planes)
        copies.append(pltpu.make_async_copy(snap_ref.at[span], rows_ref.at[span], sems.at[i]))
        copies[-1].start()
    flow = pltpu.make_async_copy(velocity_ref, flow_ref.at[:3], sems.at[steps + 1])
    flow.start()
    spread = pltpu.make_async_copy(viscosity_ref, flow_ref.at[3], sems.at[steps + 2])
    spread.start()
    table.wait()
    for i, part in enumerate(split3(table_ref[...])):
        parts_ref[i * columns : (i + 1) * columns, :] = part
    even = [flag_ref[k] == 0 for k in range(3)]
    for i in range(steps):
        copies[i].wait()
        span = slice(i * planes, (i + 1) * planes)
        rows = rows_ref[span].reshape(-1, columns)
        made = matmul(jnp.concatenate([rows, rows, rows], axis=1), parts_ref[...], 1, 0)
        made = made.astype(bf16)
        gram = matmul(made, made, 0, 0)
        for at, value in (
            (0, gram[:half, :half]),
            (half, gram[:half, half:]),
            (columns, gram[half:, half:]),
        ):
            value = value if i == 0 else gram_ref[at : at + half, :] + value
            gram_ref[at : at + half, :] = value * scale if i == steps - 1 else value
        out_ref[span] = made.reshape(planes, cells_y, cells_z, columns)
        field = out_ref[span]
        low_y, high_y = field[:, 0], field[:, cells_y - 1]
        y1_ref[span] = jnp.where(even[1], high_y, low_y)
        y2_ref[span] = jnp.where(even[1], low_y, high_y)
        low_z = field[:, :, 0, :].astype(f32)
        high_z = field[:, :, cells_z - 1, :].astype(f32)
        z1_ref[span] = jnp.where(even[2], high_z, low_z).astype(bf16)
        z2_ref[span] = jnp.where(even[2], low_z, high_z).astype(bf16)
    flow.wait()
    spread.wait()
    for k in range(4):
        for x in range(cells_x):
            plane = flow_ref[k, x].T
            coef_ref[k, x] = 0.5 * plane if k < 3 else plane
    low_x, high_x = out_ref[0], out_ref[cells_x - 1]
    x1_ref[...] = jnp.where(even[0], high_x, low_x)
    x2_ref[...] = jnp.where(even[0], low_x, high_x)
    size = sent_ref.shape[0]
    mine = pl.multiple_of(flag_ref[3] * size, size)
    other = pl.multiple_of((1 - flag_ref[3]) * size, size)
    kept_ref[...] = gram_ref[pl.ds(mine, size), :]
    sent_ref[...] = gram_ref[pl.ds(other, size), :]


def sketch_call(flags, snapshots, sketch, velocity, viscosity, scale):
    cells_x, cells_y, cells_z, columns = snapshots.shape
    half = columns // 2
    steps = 1
    return pl.pallas_call(
        functools.partial(sketch_kernel, scale, steps),
        in_specs=[SMEM] + [HBM] * 4,
        out_specs=[VMEM] * 10,
        out_shape=[
            on_chip(snapshots.shape, bf16),
            on_chip((cells_y, cells_z, columns), bf16),
            on_chip((cells_y, cells_z, columns), bf16),
            on_chip((cells_x, cells_z, columns), bf16),
            on_chip((cells_x, cells_z, columns), bf16),
            on_chip((cells_x, cells_y, columns), bf16),
            on_chip((cells_x, cells_y, columns), bf16),
            on_chip((3 * half // 2, half), f32),
            on_chip((3 * half // 2, half), f32),
            on_chip((4, cells_x, cells_z, cells_y), f32),
        ],
        scratch_shapes=[
            pltpu.VMEM(snapshots.shape, bf16),
            pltpu.VMEM(sketch.shape, f32),
            pltpu.VMEM((3 * columns, columns), bf16),
            pltpu.VMEM((3 * half, half), f32),
            pltpu.VMEM((4, cells_x, cells_y, cells_z), f32),
            pltpu.SemaphoreType.DMA((steps + 3,)),
        ],
        compiler_params=PARAMS,
        name="sketch",
    )(flags, *in_hbm(snapshots, sketch, velocity, viscosity))


def operator_kernel(
    scale,
    planes,
    flag_ref,
    s_ref,
    x1_ref,
    x2_ref,
    y1_ref,
    y2_ref,
    z1_ref,
    z2_ref,
    coef_ref,
    *refs,
):
    cells_x, cells_y, cells_z, columns = s_ref.shape
    first, last = planes[0], planes[-1]
    even = [flag_ref[k] == 0 for k in range(3)]
    if first == 0:
        image_ref, total_ref = refs
    else:
        sum_ref, image_ref, sent_ref, kept_ref, total_ref = refs
    for x in planes:
        for y in range(cells_y):
            middle = s_ref[x, y].astype(f32)
            if x > 0:
                before = s_ref[x - 1, y]
            else:
                before = jnp.where(even[0], x2_ref[y], x1_ref[y])
            if x < cells_x - 1:
                after = s_ref[x + 1, y]
            else:
                after = jnp.where(even[0], x1_ref[y], x2_ref[y])
            before, after = before.astype(f32), after.astype(f32)
            if y > 0:
                south = s_ref[x, y - 1]
            else:
                south = jnp.where(even[1], y2_ref[x], y1_ref[x])
            if y < cells_y - 1:
                north = s_ref[x, y + 1]
            else:
                north = jnp.where(even[1], y1_ref[x], y2_ref[x])
            south, north = south.astype(f32), north.astype(f32)
            z1, z2 = z1_ref[x, y : y + 1].astype(f32), z2_ref[x, y : y + 1].astype(f32)
            below, above = jnp.where(even[2], z2, z1), jnp.where(even[2], z1, z2)
            lower = jnp.concatenate([below, middle[:-1]], axis=0)
            upper = jnp.concatenate([middle[1:], above], axis=0)
            around = (after + before) + (north + south) + (upper + lower)

            def spread(k):
                return jnp.broadcast_to(coef_ref[k, x, :, y : y + 1], middle.shape)

            image = spread(3) * (6.0 * middle - around)
            image = image + spread(0) * (after - before)
            image = image + spread(1) * (north - south)
            image = image + spread(2) * (upper - lower)
            high, low = split2(image)
            at = ((x - first) * cells_y + y) * cells_z
            image_ref[at : at + cells_z, :columns] = high
            image_ref[at : at + cells_z, columns:] = low
    base = s_ref[first : last + 1].reshape(-1, columns)
    high, low = image_ref[:, :columns], image_ref[:, columns:]
    part = matmul(jnp.concatenate([base, base], axis=0), jnp.concatenate([high, low], axis=0), 0, 0)
    if first == 0:
        total_ref[...] = part
    else:
        total_ref[...] = (sum_ref[...] + part) * scale
        size = columns // 2
        mine = pl.multiple_of(flag_ref[3] * size, size)
        other = pl.multiple_of((1 - flag_ref[3]) * size, size)
        for at in (0, size):
            kept_ref[at : at + size, :] = total_ref[pl.ds(mine, size), at : at + size]
            sent_ref[at : at + size, :] = total_ref[pl.ds(other, size), at : at + size]


def operator_calls(flags, sketched, halos, coefs, scale):
    cells_x, cells_y, cells_z, columns = sketched.shape
    half = cells_x // 2
    image = on_chip((half * cells_y * cells_z, 2 * columns), bf16)
    image0, partial = pl.pallas_call(
        functools.partial(operator_kernel, scale, range(half)),
        in_specs=[SMEM] + [VMEM] * 8,
        out_specs=[VMEM] * 2,
        out_shape=[image, on_chip((columns, columns), f32)],
        compiler_params=PARAMS,
        name="operator0",
    )(flags, *held(sketched, *halos, coefs))
    image1, sent, kept = pl.pallas_call(
        functools.partial(operator_kernel, scale, range(half, cells_x)),
        in_specs=[SMEM] + [VMEM] * 9,
        out_specs=[VMEM] * 3,
        out_shape=[image] + [on_chip((columns, columns // 2), f32)] * 2,
        scratch_shapes=[pltpu.VMEM((columns, columns), f32)],
        compiler_params=PARAMS,
        name="operator1",
    )(flags, *held(sketched, *halos, coefs, partial))
    return image0, image1, sent, kept


def total(values):
    values = list(values)
    while len(values) > 1:
        pairs = zip(values[::2], values[1::2])
        values = [a + b for a, b in pairs] + values[len(values) // 2 * 2 :]
    return values[0]


def eliminate(block, cells_ref):
    size = block.shape[0]
    sub = lax.broadcasted_iota(jnp.int32, (TILE, size), 0)
    lane = lax.broadcasted_iota(jnp.int32, (TILE, size), 1)
    tiles = [block[i : i + TILE, :] for i in range(0, size, TILE)]
    count = size // TILE
    pivots = []

    def full(value):
        return jnp.broadcast_to(value, (TILE, size))

    for s in range(count):
        at = s * TILE
        tile = tiles[s]
        cols = [
            [full(tiles[t][:, at + k : at + k + 1]) for k in range(TILE)] for t in range(s, count)
        ]
        for k in range(TILE):
            cells_ref[k * TILE : (k + 1) * TILE, :] = cols[0][k]
        a = [
            [cells_ref[pl.ds(k * TILE + i, TILE, stride=0), :] for k in range(i + 1)]
            for i in range(TILE)
        ]
        w = [[None] * TILE for _ in range(TILE)]
        r = []
        for j in range(TILE):
            r.append(1.0 / a[j][j])
            m = [a[i][j] * r[j] if i > j else None for i in range(TILE)]
            for i in range(j + 1, TILE):
                for k in range(j + 1, i + 1):
                    a[i][k] = a[i][k] - m[i] * a[k][j]
                for k in range(j):
                    w[i][k] = w[i][k] - m[i] * w[j][k]
                w[i][j] = -m[i]
        unit = []
        for k in range(TILE):
            col = jnp.where(sub == k, 1.0, 0.0)
            for i in range(k + 1, TILE):
                col = jnp.where(sub == i, w[i][k], col)
            unit.append(col)
        pivot = r[0]
        for i in range(1, TILE):
            pivot = jnp.where(sub == i, r[i], pivot)
        pivots.append(pivot[:, :1])
        new = total(unit[k] * full(tile[k : k + 1, :]) for k in range(TILE))
        for k in range(TILE):
            new = jnp.where(lane == at + k, unit[k], new)
        tiles[s] = new
        if s == count - 1:
            break
        rows = [full(new[k : k + 1, :]) * r[k] for k in range(TILE)]
        inside = (lane >= at) & (lane < at + TILE)
        for t in range(s + 1, count):
            col = cols[t - s]
            terms = []
            for k in range(TILE):
                factor = total([col[k]] + [w[k][i] * col[i] for i in range(k)])
                terms.append(factor * rows[k])
            tiles[t] = jnp.where(inside, 0.0, tiles[t]) - total(terms)
    result = jnp.concatenate(tiles, axis=0)
    row_b = lax.broadcasted_iota(jnp.int32, (size, size), 0)
    lane_b = lax.broadcasted_iota(jnp.int32, (size, size), 1)
    return jnp.where(lane_b <= row_b, result, 0.0), jnp.concatenate(pivots, axis=0)


def factor_kernel(start, *refs):
    refs, cells_ref = refs[:-1], refs[-1]
    if start == 0:
        flag_ref, part_ref, other_ref, out_ref, next_ref, state_ref = refs
        half = state_ref.shape[1] // 2
        own_first = flag_ref[3] == 0
        part, other = part_ref[...], other_ref[...]
        upper = jnp.where(own_first, part, other)
        under = jnp.where(own_first, other, part)
        both = jnp.concatenate([upper, under], axis=0)
        state_ref[:half, :half] = both[:half]
        state_ref[:half, half:] = both[half : 2 * half]
        state_ref[half:, :half] = jnp.zeros((half, half), f32)
        state_ref[half:, half:] = both[2 * half :]
    elif len(refs) == 3:
        state_ref, out_ref, next_ref = refs
    else:
        state_ref, out_ref = refs
        next_ref = None
    n = state_ref.shape[1]
    end = start + PANEL
    lane = lax.broadcasted_iota(jnp.int32, (PANEL, n), 1)
    unit, pivots = eliminate(state_ref[:PANEL, start:end], cells_ref)
    panel = dot_f32(unit, state_ref[:PANEL, :], 1, 0)
    pieces = [unit]
    if start:
        pieces = [jnp.zeros((PANEL, start), f32)] + pieces
    if end < n:
        pieces = pieces + [jnp.zeros((PANEL, n - end), f32)]
    inside = (lane >= start) & (lane < end)
    rows = jnp.where(inside, jnp.concatenate(pieces, axis=1), panel)
    out_ref[...] = jnp.where(lane < end, rows * jnp.sqrt(pivots), 0.0)
    if end < n:
        factors = (panel * pivots)[:, end:]
        lane_r = lax.broadcasted_iota(jnp.int32, (n - end, n), 1)
        old = jnp.where((lane_r >= start) & (lane_r < end), 0.0, state_ref[PANEL:, :])
        next_ref[...] = old - dot_f32(factors, rows, 0, 0)


def factor_calls(flags, part, other):
    n = part.shape[1] * 2
    rows = []
    state = None
    for start in range(0, n, PANEL):
        left = n - start - PANEL
        outs = [on_chip((PANEL, n), f32)]
        if left:
            outs.append(on_chip((left, n), f32))
        args = (flags, *held(part, other)) if start == 0 else held(state)
        got = pl.pallas_call(
            functools.partial(factor_kernel, start),
            in_specs=[SMEM, VMEM, VMEM] if start == 0 else [VMEM],
            out_specs=[VMEM] * len(outs),
            out_shape=outs,
            scratch_shapes=([pltpu.VMEM((n, n), f32)] if start == 0 else [])
            + [pltpu.VMEM((TILE * TILE + TILE, PANEL), f32)],
            compiler_params=PARAMS,
        )(*args)
        rows.append(got[0])
        if left:
            state = got[1]
    return rows


def finish_kernel(steps, flag_ref, part_ref, other_ref, image0_ref, image1_ref, *refs):
    count = len(refs) - 6
    inverse_refs, rest = refs[:count], refs[count:]
    out_ref, reduced_ref, right_ref, made_ref, sum_ref, sems = rest
    columns = out_ref.shape[1]
    half = columns // 2
    inverse = jnp.concatenate([ref[...] for ref in inverse_refs], axis=0)
    own_first = flag_ref[3] == 0
    part = jnp.concatenate([part_ref[:half, :], part_ref[half:, :]], axis=1)
    other = jnp.concatenate([other_ref[:half, :], other_ref[half:, :]], axis=1)
    gram = jnp.concatenate(
        [jnp.where(own_first, part, other), jnp.where(own_first, other, part)], axis=0
    )
    high, low = split2(inverse)
    right_ref[...] = jnp.concatenate([high, low, high], axis=1)
    right = right_ref[...]
    block = out_ref.shape[0] // steps
    copies = []

    def send(source, target):
        copies.append(pltpu.make_async_copy(source, target, sems.at[len(copies)]))
        copies[-1].start()

    def applied(i):
        ref, at = (image0_ref, i) if i < steps // 2 else (image1_ref, i - steps // 2)
        image = ref[at * block : (at + 1) * block, :]
        left = jnp.concatenate([image[:, :columns], image], axis=1)
        made_ref[i * block : (i + 1) * block, :] = matmul(left, right, 1, 1).astype(bf16)

    middle = dot_f32(inverse, gram, 1, 0)
    for i in range(steps - 1):
        applied(i)
    span = pl.ds(0, (steps - 1) * block)
    send(made_ref.at[span], out_ref.at[span])
    sum_ref[...] = dot_f32(middle, inverse, 1, 1)
    applied(steps - 1)
    span = pl.ds((steps - 1) * block, block)
    send(sum_ref, reduced_ref)
    send(made_ref.at[span], out_ref.at[span])
    for copy in copies:
        copy.wait()


def finish_call(flags, part, other, image0, image1, rows):
    count, columns = image0.shape[0] * 2, image0.shape[1] // 2
    steps = 4
    return pl.pallas_call(
        functools.partial(finish_kernel, steps),
        in_specs=[SMEM] + [VMEM] * (4 + len(rows)),
        out_specs=[HBM, HBM],
        out_shape=[
            jax.ShapeDtypeStruct((count, columns), bf16),
            jax.ShapeDtypeStruct((columns, columns), f32),
        ],
        scratch_shapes=[
            pltpu.VMEM((columns, 3 * columns), bf16),
            pltpu.VMEM((count, columns), bf16),
            pltpu.VMEM((columns, columns), f32),
            pltpu.SemaphoreType.DMA((3,)),
        ],
        compiler_params=PARAMS,
        name="finish",
    )(flags, *held(part, other, image0, image1, *rows))


AXES = ("gx", "gy", "gz")
PLANE = ("gx", "gy")


def swap(value, masks):
    depth = lax.axis_size("gz")
    pairs = [(i, i ^ masks[i // depth % 2]) for i in range(lax.axis_size(AXES))]
    return lax.ppermute(value, AXES, pairs)


def stages():
    depth = lax.axis_size("gz")
    plane, line = [], []
    mask = 2
    while mask < lax.axis_size(PLANE):
        plane.append(mask * depth)
        mask *= 2
    mask = 1
    while mask < depth:
        line.append(mask)
        mask *= 2
    bits = line[-1:] + plane + line[:-1]
    turned = list(bits)
    for k in range(0, len(bits) - 1, 2):
        turned[k], turned[k + 1] = bits[k + 1], bits[k]
    return list(zip(bits, turned))


def exchange(part, masks):
    got = swap(part, masks)
    return part + got


def trade(sent):
    depth = lax.axis_size("gz")
    return swap(sent, (depth, depth))


def halo_pair(first, second, axis):
    count = lax.axis_size(axis)
    got = []
    for start, layer in ((0, first), (1, second)):
        pairs = []
        for i in range(start, count - 1, 2):
            pairs += [(i, i + 1), (i + 1, i)]
        if pairs:
            got.append(lax.ppermute(layer, axis, pairs))
        else:
            got.append(jnp.zeros_like(layer))
    return got


def body(snapshots, sketch, velocity, viscosity):
    shape = snapshots.shape
    ncells = shape[0] * shape[1] * shape[2]
    for axis in ("gx", "gy", "gz"):
        ncells *= lax.axis_size(axis)
    scale = 1.0 / ncells
    flags = [lax.axis_index(axis) % 2 for axis in ("gx", "gy", "gz")]
    flags = jnp.stack(flags + [lax.axis_index(PLANE) % 2]).astype(jnp.int32)
    sketched, x1, x2, y1, y2, z1, z2, sent, kept, coefs = sketch_call(
        flags, snapshots, sketch, velocity, viscosity, scale
    )
    steps = stages()
    part = kept + trade(sent)
    for masks in steps:
        part = exchange(part, masks)
    other = trade(part)
    halos = halo_pair(x1, x2, "gx") + halo_pair(y1, y2, "gy")
    halos = halos + halo_pair(z1, z2, "gz")
    image0, image1, sent, kept = operator_calls(flags, sketched, halos, coefs, scale)
    i_part = kept + trade(sent)
    turn = [3, 0, 1, 2] if len(steps) == 4 else range(len(steps))
    for stage in turn:
        i_part = exchange(i_part, steps[stage])
    i_other = trade(i_part)
    rows = factor_calls(flags, part, other)
    applied, reduced = finish_call(flags, i_part, i_other, image0, image1, rows)
    return applied.reshape(shape), reduced


def solution(mesh):
    in_specs = (P("gx", "gy", "gz", None), P(), P(None, "gx", "gy", "gz"), P("gx", "gy", "gz"))
    out_specs = (P("gx", "gy", "gz", None), P())
    return jax.shard_map(body, mesh=mesh, in_specs=in_specs, out_specs=out_specs, check_vma=False)
```
